512 devices in a mesh: segment: 8 (over y, core), band: 16 (over z), dp: 4 (over x).
Axes of the slice: x: 4, y: 4, z: 16, core: 2. Of those that a mesh axis runs over, the one named last changes fastest.
Arguments:
- latents: bfloat16 [8, 64, 16, 320], P('dp', 'band'), may hold values from -6 to 6
- hint_field: bfloat16 [8, 64, 16, 320], P('dp', 'band'), may hold values from -6 to 6
- weights: bfloat16 [8, 3200, 320], P('segment'), may hold values from -0.109375 to 0.109375
- cotangent: bfloat16 [8, 64, 16, 320], P('dp', 'band'), may hold values from -0.06591797 to 0.06591797
Outputs:
- grad_weights: float32 [8, 3200, 320], P('segment', ('band', 'dp'))
The draws below stay inside these ranges and needn't reach their ends.
All inputs are finite; a program needn't handle non-finite values.
Results may differ from the reference program's by a relative error of at most 0.019.
Values may be sent and summed in bfloat16 or wider, within the bound.
No kernel may reach another device: no remote copies, remote signals or barrier semaphores. Data moves between devices by JAX's collectives and lax.ppermute only.
A program may use at most 64 MiB of HBM per device.

```python
import jax
import jax.numpy as jnp
from jax import lax

C = 320
WIDTH = 16
NC = 4
ND = 3
LAYERS = 8
BATCH = 8
HEIGHT = 64


def block_levels(rng, shape, shards, smallest, high):
    loudness, own = 1.0, jax.random.fold_in(rng, 6)
    for dim, shards_of in shards:
        heights = jnp.exp(jax.random.uniform(jax.random.fold_in(own, dim), (shards_of,), jnp.float32, smallest / len(shards), high / len(shards)))
        loudness = loudness * jnp.repeat(heights, shape[dim] // shards_of).reshape([-1 if axis == dim else 1 for axis in range(len(shape))])
    return loudness


def scatter_about(stream_key, shape, width, most, cuts=(), dtype=jnp.bfloat16):
    entries = jax.random.normal(stream_key, shape, jnp.float32) * width
    if len(cuts) > 0:
        entries = block_levels(stream_key, shape, cuts, -0.22, 0.18) * entries
    return jnp.clip(entries, min=-most, max=most).astype(dtype)


def setup_inputs(seed: int = 0) -> dict:
    keys = jax.random.split(jax.random.key(seed), 5)
    return {
        "latents": scatter_about(keys[0], (BATCH, HEIGHT, WIDTH, C), 1.0, 6.0, ((0, 4), (1, 16))),
        "hint_field": scatter_about(keys[1], (BATCH, HEIGHT, WIDTH, C), 1.0, 6.0, ((0, 4), (1, 16))),
        "weights": scatter_about(keys[2], (LAYERS, 10 * C, C), (9 * C) ** -0.5, 0.109375, ((0, 8),)),
        "cotangent": scatter_about(keys[3], (BATCH, HEIGHT, WIDTH, C), ((BATCH * HEIGHT * WIDTH) ** -0.5), 0.06591797, ((0, 4), (1, 16))),
    }


def silu_grad(inputs):
    sigmoid_value = jax.nn.sigmoid(inputs)
    return sigmoid_value * (1.0 + inputs * (1.0 - sigmoid_value))

def conv_forward(padded, conv_weight, height):
    breadth = padded.shape[1] - 2
    channels = padded.shape[2]
    summed = jnp.zeros((height * breadth, channels), jnp.float32)
    for i in range(3):
        for j in range(3):
            section = padded[i:i + height, j:j + breadth].reshape(height * breadth, channels)
            tap_weight = conv_weight[(3 * i + j) * channels:(3 * i + j + 1) * channels]
            summed = summed + jnp.dot(section, tap_weight, preferred_element_type=jnp.float32)
    return summed.reshape(height, breadth, channels)

def conv_back(padded, conv_weight, height):
    breadth = padded.shape[1] - 2
    channels = padded.shape[2]
    summed = jnp.zeros((height * breadth, channels), jnp.float32)
    for i in range(3):
        for j in range(3):
            section = padded[2 - i:2 - i + height, 2 - j:2 - j + breadth].reshape(height * breadth, channels)
            tap_weight = conv_weight[(3 * i + j) * channels:(3 * i + j + 1) * channels]
            summed = summed + lax.dot_general(section, tap_weight, (((1,), (1,)), ((), ())), preferred_element_type=jnp.float32)
    return summed.reshape(height, breadth, channels)

def conv_grads(padded, grad_rows, height):
    breadth = padded.shape[1] - 2
    channels = padded.shape[2]
    flat_grad = grad_rows.reshape(height * breadth, channels)
    blocks = []
    for i in range(3):
        for j in range(3):
            section = padded[i:i + height, j:j + breadth].reshape(height * breadth, channels)
            blocks.append(lax.dot_general(section, flat_grad, (((0,), (0,)), ((), ())), preferred_element_type=jnp.float32))
    return jnp.concatenate(blocks, 0)

def pad_image(field_rows):
    return jnp.pad(field_rows, ((1, 1), (1, 1), (0, 0)))

def layer_step(before, conv_weight):
    silu_in = jax.nn.silu(before.astype(jnp.float32)).astype(jnp.bfloat16)
    padded = pad_image(silu_in)
    result = (before.astype(jnp.float32) + conv_forward(padded, conv_weight, before.shape[0])).astype(jnp.bfloat16)
    return (padded, result)

def reference(latents, hint_field, weights, cotangent):
    channels = latents.shape[3]
    conv_rows = 9 * channels
    layer_count = 1 + NC + ND

    def one_image(grad_sums, inputs):
        latent, hint_map, grad_out = inputs
        height = latent.shape[0]
        unused, skip_field = layer_step(latent, weights[0, :conv_rows])
        active = (latent.astype(jnp.float32) + hint_map.astype(jnp.float32)).astype(jnp.bfloat16)
        zero_sum = jnp.zeros(latent.shape, jnp.bfloat16)
        control_saved = []
        for layer_index in range(1, NC + 1):
            padded, result = layer_step(active, weights[layer_index, :conv_rows])
            zero_term = jnp.dot(result.reshape(-1, channels), weights[layer_index, conv_rows:], preferred_element_type=jnp.float32)
            zero_sum = (zero_sum.astype(jnp.float32) + zero_term.reshape(latent.shape)).astype(jnp.bfloat16)
            control_saved.append((active, padded, result))
            active = result
        active = (skip_field.astype(jnp.float32) + zero_sum.astype(jnp.float32)).astype(jnp.bfloat16)
        decoder_saved = []
        for layer_index in range(NC + 1, layer_count):
            padded, result = layer_step(active, weights[layer_index, :conv_rows])
            decoder_saved.append(active)
            active = result
        grad_here = grad_out
        for offset in reversed(range(ND)):
            layer_index = NC + 1 + offset
            before = decoder_saved[offset]
            spread = conv_back(pad_image(grad_here), weights[layer_index, :conv_rows], height)
            grad_here = (grad_here.astype(jnp.float32) + silu_grad(before.astype(jnp.float32)) * spread).astype(jnp.bfloat16)
        grad_join = grad_here
        join_flat = grad_join.reshape(-1, channels)
        grad_here = jnp.zeros(latent.shape, jnp.bfloat16)
        layer_grads = [None] * NC
        for offset in reversed(range(NC)):
            layer_index = 1 + offset
            before, padded, result = control_saved[offset]
            zero_weight = weights[layer_index, conv_rows:]
            zero_term = lax.dot_general(join_flat, zero_weight, (((1,), (1,)), ((), ())), preferred_element_type=jnp.float32)
            effective = (grad_here.astype(jnp.float32) + zero_term.reshape(latent.shape)).astype(jnp.bfloat16)
            kernel_grad = conv_grads(padded, effective, height)
            zero_grad = lax.dot_general(result.reshape(-1, channels), join_flat, (((0,), (0,)), ((), ())), preferred_element_type=jnp.float32)
            layer_grads[offset] = jnp.concatenate([kernel_grad, zero_grad], 0)
            spread = conv_back(pad_image(effective), weights[layer_index, :conv_rows], height)
            grad_here = (effective.astype(jnp.float32) + silu_grad(before.astype(jnp.float32)) * spread).astype(jnp.bfloat16)
        empty_grad = jnp.zeros((10 * channels, channels), jnp.float32)
        stacked = jnp.stack([empty_grad] + layer_grads + [empty_grad] * ND, 0)
        return (grad_sums + stacked, None)
    initial = jnp.zeros((layer_count, 10 * channels, channels), jnp.float32)
    scanned = lax.scan(one_image, initial, (latents, hint_field, cotangent))
    return scanned[0]
```

```python
import jax
import jax.numpy as jnp
from jax import lax
from jax.experimental import pallas as pl
from jax.experimental.pallas import tpu as pltpu
from jax.sharding import PartitionSpec as P

AXES = ("segment", "band", "dp")
C = 320
TAPS = 9 * C
BF = jnp.bfloat16
F32 = jnp.float32
GATHER = {1: 0, 2: 3, 3: 7, 4: 5}


def silu(v):
    v = v.astype(F32)
    return v * jax.nn.sigmoid(v)


def silu_grad(v):
    v = v.astype(F32)
    s = jax.nn.sigmoid(v)
    return s * (1.0 + v * (1.0 - s))


def rounded(v):
    return v.astype(BF)


def columns(u):
    shape = u.shape
    flat = u.astype(F32).reshape(-1, C)
    rows = flat.shape[0]
    x = lax.broadcasted_iota(jnp.int32, flat.shape, 0) % 16
    left = jnp.where(x == 0, 0.0, pltpu.roll(flat, 1, 0))
    right = jnp.where(x == 15, 0.0, pltpu.roll(flat, rows - 1, 0))
    return tuple(rounded(f).reshape(shape) for f in (left, flat, right))


def by_offset(u, seam):
    sides = columns(u)
    if seam is None:
        return (sides,) * 3
    start, cut = seam
    row = lax.broadcasted_iota(jnp.int32, u.shape, 1) + start
    above = tuple(rounded(jnp.where(cut & (row == 3), 0.0, s.astype(F32))) for s in sides)
    below = tuple(rounded(jnp.where(cut & (row == 4), 0.0, s.astype(F32))) for s in sides)
    return above, sides, below


def conv(u, w_ref, seam=None):
    n, rows = u.shape[0], u.shape[1] - 2
    fields = by_offset(u, seam)
    out = None
    for i in range(3):
        for j in range(3):
            part = fields[i][j][:, i : i + rows].reshape(-1, C)
            tap = 3 * i + j
            term = lax.dot_general(
                part,
                w_ref[:, tap * C : (tap + 1) * C],
                (((1,), (1,)), ((), ())),
                preferred_element_type=F32,
            )
            out = term if out is None else out + term
    return out.reshape(n, rows, 16, C)


def conv_t(g, w_ref, seam=None):
    n, rows = g.shape[0], g.shape[1] - 2
    fields = by_offset(g, seam)
    out = None
    for i in range(3):
        for j in range(3):
            part = fields[2 - i][2 - j][:, 2 - i : 2 - i + rows].reshape(-1, C)
            tap = 3 * i + j
            term = jnp.dot(
                part, w_ref[:, tap * C : (tap + 1) * C], preferred_element_type=F32
            )
            out = term if out is None else out + term
    return out.reshape(n, rows, 16, C)


def zero_conv(v, w_ref):
    out = lax.dot_general(
        v.reshape(-1, C),
        w_ref[:, TAPS:],
        (((1,), (1,)), ((), ())),
        preferred_element_type=F32,
    )
    return out.reshape(v.shape)


def zero_conv_t(g, z):
    out = jnp.dot(g.reshape(-1, C), z, preferred_element_type=F32)
    return out.reshape(g.shape)


def inside(v, first, band):
    row = lax.broadcasted_iota(jnp.int32, v.shape, 1) + (4 * band + first)
    return jnp.where((row >= 0) & (row < 64), v.astype(F32), 0.0)


def layer(v, w_ref, seam=None):
    out = conv(rounded(silu(v)), w_ref, seam)
    return v[:, 1:-1].astype(F32) + out


def whole(m, u, d):
    m, u, d = m.astype(F32), u.astype(F32), d.astype(F32)
    return jnp.concatenate(
        [
            u[:, 0:1],
            u[:, 1:2] + m[:, 0:1],
            u[:, 2:3] + m[:, 1:2],
            m[:, 2:4],
            m[:, 4:5] + d[:, 0:1],
            m[:, 5:6] + d[:, 1:2],
            d[:, 2:3],
        ],
        axis=1,
    )


def k_first(at, lat_h, hint_h, cot_h, w_h, m, u, d, sm, lat, hint, cot, w, sems):
    seg = at[0]
    pairs = ((lat_h, lat), (hint_h, hint), (cot_h, cot), (w_h, w))
    copies = [pltpu.make_async_copy(a, b, sems.at[k]) for k, (a, b) in enumerate(pairs)]

    @pl.when(seg == 5)
    def _():
        copies[2].start()
        copies[2].wait()
        u[:, 0:2] = cot[:, 2:4]
        d[:, 0:2] = cot[:, 0:2]

    @pl.when((seg <= 1) | (seg == 3))
    def _():
        copies[0].start()
        copies[1].start()

        @pl.when(seg <= 1)
        def _():
            copies[3].start()

        copies[0].wait()
        copies[1].wait()

    @pl.when(seg == 3)
    def _():
        start = rounded(lat[...].astype(F32) + hint[...].astype(F32))
        u[:, 0:2] = start[:, 2:4]
        d[:, 0:2] = start[:, 0:2]

    @pl.when(seg <= 1)
    def _():
        start = rounded(lat[...].astype(F32) + hint[...].astype(F32))
        v = jnp.where(seg == 0, lat[...].astype(F32), start.astype(F32))
        none = jnp.zeros((2, 1, 16, C), F32)
        none2 = jnp.zeros((2, 2, 16, C), F32)
        act = rounded(jnp.concatenate([none2, silu(v), none2], axis=1))
        copies[3].wait()
        part = conv(act, w) + jnp.concatenate([none, v, none], axis=1)
        part = rounded(part)

        @pl.when(seg == 0)
        def _():
            sm[...] = part[:, 2:6]
            d[...] = part[:, 0:4]

        @pl.when(seg == 1)
        def _():
            term = rounded(zero_conv(part, w))
            m[:, 0:6] = part
            m[:, 6:10] = term[:, 1:5]
            u[:, 0:3] = part[:, 3:6]
            u[:, 3:4] = term[:, 5:6]
            d[:, 0:3] = part[:, 0:3]
            d[:, 3:4] = term[:, 0:1]


def k_control_a(at, pm, pu, pd, wa, wb, c1o, c2o, c3o, hm):
    seg, band = at[0], at[1]

    @pl.when(seg == 2)
    def _():
        m, u = pm[...], pu[...]
        d = jnp.where(band == 15, 0.0, pd[...].astype(F32))
        c1 = rounded(inside(whole(m[:, 0:6], u[:, 0:3], d[:, 0:3]), -2, band))
        t1 = jnp.concatenate(
            [
                m[:, 6:7].astype(F32) + u[:, 3:4].astype(F32),
                m[:, 7:9].astype(F32),
                m[:, 9:10].astype(F32) + d[:, 3:4].astype(F32),
            ],
            axis=1,
        )
        c2 = rounded(inside(layer(c1, wa), -1, band))
        c3 = rounded(layer(c2, wb))
        joint = rounded(t1 + zero_conv(c2[:, 1:5], wa) + zero_conv(c3, wb))
        c1o[...] = c1
        c2o[...] = c2
        c3o[...] = c3
        hm[:, 0:4] = c3
        hm[:, 4:8] = joint


def k_control_b(at, pm, pd, sm, sd, c1i, wa, wb, c3o, jo, fo, om):
    seg, band = at[0], at[1]

    @pl.when(seg == 2)
    def _():
        fo[:, 6:10] = c1i[:, 2:6]

    @pl.when(seg == 4)
    def _():
        last = band == 15
        c3 = jnp.concatenate([pm[:, 0:4], pd[:, 0:4]], axis=1)
        sums = jnp.concatenate([pm[:, 5:8], pd[:, 4:7]], axis=1)
        m, d = sm[...].astype(F32), sd[...].astype(F32)
        skip = jnp.concatenate(
            [
                m[:, 0:2],
                m[:, 2:3] + jnp.where(last, 0.0, d[:, 0:1]),
                d[:, 1:2] + jnp.where(last, 0.0, m[:, 3:4]),
                d[:, 2:4],
            ],
            axis=1,
        )
        c4 = rounded(layer(c3, wa, (0, last)))
        joined = rounded(rounded(skip).astype(F32) + sums.astype(F32) + zero_conv(c4, wa))
        c3o[...] = c3
        jo[...] = joined
        fo[:, 0:6] = c3[:, 1:7]
        fo[:, 6:10] = c4[:, 1:5]
        om[...] = rounded(layer(joined, wb, (1, last)))


def k_turn(at, pm, pu, cot, cu, cd, wa, wb, gm):
    seg, band = at[0], at[1]

    @pl.when(seg == 6)
    def _():
        v6 = jnp.concatenate([pu[...], pm[...]], axis=1)
        v6 = rounded(inside(v6, -2, band))
        grad = jnp.concatenate([cu[:, 0:2], cot[...], cd[:, 0:2]], axis=1)
        grad = rounded(inside(grad, -2, band))
        v7 = rounded(layer(v6, wa))
        g6 = grad[:, 1:7].astype(F32) + silu_grad(v7) * conv_t(grad, wb)
        g6 = rounded(inside(g6, -1, band))
        g5 = g6[:, 1:5].astype(F32) + silu_grad(v6[:, 2:6]) * conv_t(g6, wa)
        gm[...] = rounded(g5)


def k_back_b(at, pm, pd, c3i, ji, wa, wb, eo, hm):
    seg, band = at[0], at[1]

    @pl.when(seg == 4)
    def _():
        last = band == 15
        g5 = jnp.concatenate([pm[...], pd[...]], axis=1)
        joined, c3 = ji[...], c3i[...]
        gj = g5[:, 1:7].astype(F32) + silu_grad(joined) * conv_t(g5, wb, (0, last))
        gj = rounded(gj)
        eff = rounded(zero_conv_t(gj, wa[:, TAPS:]))
        own = eff[:, 1:5]
        g3 = own.astype(F32) + silu_grad(c3[:, 2:6]) * conv_t(eff, wa, (1, last))
        own_j = gj[:, 1:5]
        eo[:, 0:4] = own
        eo[:, 4:8] = own_j
        hm[:, 0:4] = rounded(g3)
        hm[:, 4:8] = own_j


def k_back_a(at, pm, pu, c1i, c2i, e4, wa, wb, e1, e2, e3):
    seg, band = at[0], at[1]

    @pl.when(seg == 4)
    def _():
        e1[...] = e4[...]

    @pl.when(seg == 2)
    def _():
        g3 = jnp.concatenate([pu[:, 0:4], pm[:, 0:4]], axis=1)
        gj = jnp.concatenate([pu[:, 4:8], pm[:, 4:8]], axis=1)
        gj = rounded(inside(gj, -2, band))
        c1, c2 = c1i[...], c2i[...]
        eff3 = inside(g3.astype(F32) + zero_conv_t(gj, wb[:, TAPS:]), -2, band)
        eff3 = rounded(eff3)
        g2 = eff3[:, 1:7].astype(F32) + silu_grad(c2) * conv_t(eff3, wb)
        eff2 = rounded(g2).astype(F32) + zero_conv_t(gj[:, 1:7], wa[:, TAPS:])
        eff2 = rounded(inside(eff2, -1, band))
        g1 = eff2[:, 1:5].astype(F32) + silu_grad(c1[:, 2:6]) * conv_t(eff2, wa)
        own_j = gj[:, 2:6]
        e1[:, 0:4] = rounded(g1)
        e1[:, 4:8] = own_j
        e2[:, 0:4] = eff2[:, 1:5]
        e2[:, 4:8] = own_j
        e3[:, 0:4] = eff3[:, 2:6]
        e3[:, 4:8] = own_j


def k_gathered(at, f1, f2, f3, lat, hint, hu, hd, out):
    seg, band = at[0], at[1]

    @pl.when(seg == GATHER[1])
    def _():
        out[:, 0:1] = hu[:, 1:2]
        out[:, 1:5] = rounded(lat[...].astype(F32) + hint[...].astype(F32))
        out[:, 5:6] = rounded(jnp.where(band == 15, 0.0, hd[:, 0:1].astype(F32)))
        out[:, 6:10] = f1[:, 6:10]

    @pl.when(seg == GATHER[4])
    def _():
        out[...] = f1[...]

    @pl.when(seg == GATHER[2])
    def _():
        out[...] = f2[...]

    @pl.when(seg == GATHER[3])
    def _():
        out[...] = f3[...]


def k_picked(at, e1, e2, e3, out):
    seg = at[0]

    @pl.when((seg == GATHER[1]) | (seg == GATHER[4]))
    def _():
        out[...] = e1[...]

    @pl.when(seg == GATHER[2])
    def _():
        out[...] = e2[...]

    @pl.when(seg == GATHER[3])
    def _():
        out[...] = e3[...]


def k_weights(at, f0, f1, f2, f3, e0, e1, e2, e3, z, *outs):
    pieces, acc = outs[:16], outs[16]
    seg, band, dp = at[0], at[1], at[2]

    @pl.when((seg == 0) | (seg == 3) | (seg == 5) | (seg == 7))
    def _():
        f = jnp.concatenate([f0[...], f1[...], f2[...], f3[...]], axis=0)
        e = jnp.concatenate([e0[...], e1[...], e2[...], e3[...]], axis=0)
        act = rounded(silu(f[:, 0:6]))
        gj = e[:, 4:8].reshape(-1, C)
        first = e[:, 0:4].reshape(-1, C)
        extra = jnp.where(seg == GATHER[1], zero_conv_t(gj, z[...]), 0.0)
        eff = rounded(first.astype(F32) + extra)
        cut = (seg == GATHER[4]) & (band == 15)
        fields = by_offset(act, (1, cut))
        dims = (((0,), (0,)), ((), ()))
        for i in range(3):
            for j in range(3):
                part = fields[i][j][:, i : i + 4].reshape(-1, C)
                tap = 3 * i + j
                acc[tap * C : (tap + 1) * C, :] = lax.dot_general(
                    part, eff, dims, preferred_element_type=F32
                )
        acc[TAPS : TAPS + C, :] = lax.dot_general(
            f[:, 6:10].reshape(-1, C), gj, dims, preferred_element_type=F32
        )
        for k in range(4):

            @pl.when(dp == k)
            def _():
                base, skew = (50 * k) // 8 * 8, (50 * k) % 8
                for dz in range(16):
                    row = 200 * lax.rem(band + dz, 16) + base
                    rows = acc[pl.ds(pl.multiple_of(row, 8), 56), :]
                    pieces[dz][...] = rounded(rows[skew : skew + 50])


def place(segment, band, dp):
    return (segment * 16 + band) * 4 + dp


def moves(routes, dz=0, dx=0, around=False):
    pairs = []
    for source, target in routes:
        for z in range(16):
            to = z + dz
            if around:
                to %= 16
            if 0 <= to < 16:
                for x in range(4):
                    pairs.append((place(source, z, x), place(target, to, (x + dx) % 4)))
    return pairs


def send(value, routes, dz=0, dx=0, around=False):
    return lax.ppermute(value, AXES, moves(routes, dz, dx, around))


def field(rows, images=2):
    return jax.ShapeDtypeStruct((images, rows, 16, C), BF)


def run(body, name, out_shape, at, *args, scratch=(), after=(), limit=20, loose=False):
    vmem = pl.BlockSpec(memory_space=pltpu.VMEM)
    single = not isinstance(out_shape, (list, tuple))
    count = 1 + len(args)
    place_in = pl.BlockSpec(memory_space=pltpu.HBM) if loose else vmem

    def kernel(*refs):
        body(*refs[:count], *refs[count + len(after) :])

    return pl.pallas_call(
        kernel,
        name=name,
        out_shape=out_shape,
        in_specs=[pl.BlockSpec(memory_space=pltpu.SMEM)]
        + [place_in] * len(args)
        + [pl.BlockSpec(memory_space=pl.ANY)] * len(after),
        out_specs=vmem if single else [vmem] * len(out_shape),
        scratch_shapes=list(scratch),
        compiler_params=pltpu.CompilerParams(vmem_limit_bytes=limit << 20),
        cost_estimate=pl.CostEstimate(flops=2**31, bytes_accessed=2**22, transcendentals=0),
    )(at, *args, *after)


def shards(latents, hint_field, weights, cotangent):
    at = jnp.stack([lax.axis_index(a) for a in AXES]).astype(jnp.int32)
    own = weights[0].T
    partner = send(own, [(3, 2), (5, 4), (7, 6)])

    m, u, d, sm = run(
        k_first, "first", [field(10), field(4), field(4), field(4)],
        at, latents, hint_field, cotangent, own,
        scratch=[pltpu.VMEM((2, 4, 16, C), BF)] * 3
        + [pltpu.VMEM((C, 3200), BF), pltpu.SemaphoreType.DMA((4,))],
        loose=True, limit=61,
    )
    own, latents, hint_field, cotangent, sm, m = lax.optimization_barrier(
        (own, latents, hint_field, cotangent, sm, m)
    )
    halo = [(1, 2), (3, GATHER[1]), (5, 6)]
    pm = send(m, [(1, 2)])
    pd = send(d, halo + [(0, 4)], -1, 0, True)
    pu = send(u, halo, 1)
    sm = send(sm, [(0, 4)])

    c1, c2, c3, m = run(
        k_control_a, "control_a", [field(8), field(6), field(4), field(8)],
        at, pm, pu, pd, own, partner,
    )
    qm, qd = send(m, [(2, 4)]), send(m, [(2, 4)], -1, 0, True)
    f2 = jnp.concatenate([c1[:, 1:7], c2[:, 1:5]], axis=1)
    f3 = jnp.concatenate([c2, c3], axis=1)

    c3e, joined, f1, m = run(
        k_control_b, "control_b", [field(8), field(6), field(10), field(4)],
        at, qm, qd, sm, pd, c1, own, partner,
    )
    om, ou = send(m, [(4, 6)]), send(m, [(4, 6)], 1, 0, True)
    z1, _ = lax.optimization_barrier((own[:, TAPS:], f1))
    z1 = send(z1, [(1, GATHER[1])])
    f1 = send(f1, [(2, GATHER[1]), (4, GATHER[4])])
    f2 = send(f2, [(2, GATHER[2])])
    f3 = send(f3, [(2, GATHER[3])])

    m = run(
        k_turn, "turn", field(4), at, om, ou, cotangent, pu, pd, own, partner,
    )
    gm, gd = send(m, [(6, 4)]), send(m, [(6, 4)], -1, 0, True)
    f = run(
        k_gathered, "gathered", field(10),
        at, f1, f2, f3, latents, hint_field, pu, pd, after=[m],
    )
    ring = [(s, s) for s in GATHER.values()]
    fs = [f] + [send(f, ring, 0, dx) for dx in (1, 2, 3)]

    e4, m = run(
        k_back_b, "back_b", [field(8), field(8)],
        at, gm, gd, c3e, joined, own, partner, after=fs,
    )
    hm, hu = send(m, [(4, 2)]), send(m, [(4, 2)], 1, 0, True)
    e1, e2, e3 = run(
        k_back_a, "back_a", [field(8)] * 3,
        at, hm, hu, c1, c2, e4, own, partner,
    )
    e1 = send(e1, [(2, GATHER[1]), (4, GATHER[4])])
    e2 = send(e2, [(2, GATHER[2])])
    e3 = send(e3, [(2, GATHER[3])])
    e = run(k_picked, "picked", field(8), at, e1, e2, e3)
    es = [e] + [send(e, ring, 0, dx) for dx in (1, 2, 3)]

    pieces = run(
        k_weights, "weights", [jax.ShapeDtypeStruct((50, C), BF)] * 16,
        at, *fs, *es, z1,
        scratch=[pltpu.VMEM((3200, C), F32)],
    )
    back = [(g, l) for l, g in GATHER.items()]
    order = sorted(range(16), key=lambda dz: -min(dz, 16 - dz))
    parts = [send(pieces[dz], back, dz, 0, True) for dz in order]
    total = parts[0].astype(F32)
    for p in parts[1:]:
        total = total + p.astype(F32)
    return total[None]


def solution(mesh):
    in_specs = (
        P("dp", "band", None, None),
        P("dp", "band", None, None),
        P("segment", None, None),
        P("dp", "band", None, None),
    )
    out_specs = P("segment", ("band", "dp"), None)
    return jax.shard_map(
        shards, mesh=mesh, in_specs=in_specs, out_specs=out_specs, check_vma=False
    )
```
